256 devices in a mesh: row: 8 (over y, z_lo), col: 32 (over z_hi, x, core).
Axes of the slice: x: 4, y: 4, z: 8 (z_hi: 4, z_lo: 2; z = z_hi * 2 + z_lo), core: 2. Of those that a mesh axis runs over, the one named last changes fastest.
Arguments:
- a_tiles: float32 [16384, 16384], P('row', 'col'), as said below
- reflectors: float32 [16384, 512], P(('row', 'col'))
- t_blocks: float32 [2, 256, 256], replicated, as said below
Outputs:
- updated: float32 [16384, 16384], P('row', 'col')
- w_panel: float32 [16384, 512], P(('row', 'col'))
Inputs may be any that keep to these rules, and one draw needn't show every extreme that they name: a_tiles stores a symmetric matrix. `t_blocks`: both blocks are upper triangular with positive diagonals.
All inputs are finite; a program needn't handle non-finite values.
Results may differ from the reference program's by a relative error of at most 0.0003.
Values sent between devices are 32-bit elements; how exact they have to be, the bound alone decides.
No kernel may reach another device: no remote copies, remote signals or barrier semaphores. Data moves between devices by JAX's collectives and lax.ppermute only.
A program may use at most 64 MiB of HBM per device.

```python
import math
import jax
import jax.numpy as jnp
from jax import lax

M = 16384
PW = 256
B = 256
N_ROW = 8
N_COL = 32


def draw_a_tiles(key, part):
    noise = jax.random.normal(key, (M, M), jnp.float32)
    sym = (noise + noise.T) * 0.7071
    sym = sym.reshape(M // B // N_ROW, N_ROW, B, M).transpose(1, 0, 2, 3).reshape(M, M)
    sym = sym.reshape(M, M // B // N_COL, N_COL, B).transpose(0, 2, 1, 3).reshape(M, M)
    return sym


def draw_reflectors(key, part):
    values = jax.random.normal(key, (M, 2 * PW), jnp.float32) * (2.0 / math.sqrt(M))
    return values


def draw_t_blocks(key, part):
    diag_vals = jnp.exp(jax.random.uniform(jax.random.fold_in(key, 13), (2, PW), jnp.float32, math.log(0.5), math.log(2.0)))
    upper = jax.random.normal(jax.random.fold_in(key, 14), (2, PW, PW), jnp.float32) * (0.5 / math.sqrt(PW))
    upper = jnp.triu(upper, 1)
    eye_mat = jnp.eye(PW, dtype=jnp.float32)
    return upper + diag_vals[:, :, None] * eye_mat[None, :, :]


def setup_inputs(seed: int = 0) -> dict:
    streams_of = jax.random.split(jax.random.key(seed), 4)
    a_tiles = draw_a_tiles(jax.random.fold_in(streams_of[3], 71), 0)
    reflectors = draw_reflectors(jax.random.fold_in(streams_of[3], 71), 0)
    t_blocks = draw_t_blocks(jax.random.fold_in(streams_of[3], 71), 0)
    return {"a_tiles": a_tiles, "reflectors": reflectors, "t_blocks": t_blocks}


def matmul(left_side, right_side):
    return jnp.dot(left_side, right_side, precision=lax.Precision.HIGHEST, preferred_element_type=jnp.float32)


def column_order(rows_stored):
    rows_group = M // B // N_ROW
    cols_group = M // B // N_COL
    depth = rows_stored.shape[1]
    natural = rows_stored.reshape(N_ROW, rows_group, B, depth).transpose(1, 0, 2, 3).reshape(M, depth)
    return natural.reshape(cols_group, N_COL, B, depth).transpose(1, 0, 2, 3).reshape(M, depth)


def reference(a_tiles, reflectors, t_blocks):
    panel_width = t_blocks.shape[1]
    v_cols = column_order(reflectors)
    y_rows = matmul(a_tiles, v_cols)
    cross_gram = matmul(reflectors[:, :panel_width].T, reflectors[:, panel_width:])
    first_block = t_blocks[0]
    second_block = t_blocks[1]
    corner = -matmul(matmul(first_block, cross_gram), second_block)
    t_merged = jnp.concatenate([jnp.concatenate([first_block, corner], 1),
                                jnp.concatenate([jnp.zeros_like(second_block), second_block], 1)], 0)
    x_rows = matmul(y_rows, t_merged)
    coupling = matmul(t_merged.T, matmul(reflectors.T, x_rows))
    w_panel = x_rows - 0.5 * matmul(reflectors, coupling)
    w_cols = column_order(w_panel)
    left_factors = jnp.concatenate([w_panel, reflectors], 1).reshape(N_ROW, M // N_ROW, 4 * panel_width)
    right_factors = jnp.concatenate([v_cols, w_cols], 1)
    blocks = a_tiles.reshape(N_ROW, M // N_ROW, M)

    def one_block(pair):
        block, lefts = pair
        return block - lax.dot_general(lefts, right_factors, (((1,), (1,)), ((), ())),
                                       precision=lax.Precision.HIGHEST, preferred_element_type=jnp.float32)

    updated = lax.map(one_block, (blocks, left_factors)).reshape(M, M)
    return updated, w_panel
```

```python
import jax
import jax.numpy as jnp
from jax import lax
from jax.experimental import pallas as pl
from jax.experimental.pallas import tpu as pltpu
from jax.sharding import PartitionSpec as P

ROWS = 8
COLS = 32
CH = 64
W2 = 512
F32 = jnp.float32
BF16 = jnp.bfloat16
ANY = pl.ANY


def split(value):
    high = value.astype(BF16)
    low = (value - high.astype(F32)).astype(BF16)
    return high, low


def mm3(left, right, dims):
    lh, ll = split(left)
    rh, rl = split(right)

    def dot(a, b):
        return lax.dot_general(a, b, (dims, ((), ())), preferred_element_type=F32)

    return dot(lh, rl) + dot(ll, rh) + dot(lh, rh)


NN = ((1,), (0,))
NT = ((1,), (1,))
TN = ((0,), (0,))


def shift_row(s):
    return [(k, (k + s) % ROWS) for k in range(ROWS)]


def shift_zhi(s):
    return [(k, (k // 8 + s) % 4 * 8 + k % 8) for k in range(COLS)]


def shift_x(s):
    return [(k, k // 8 * 8 + (k // 2 % 4 + s) % 4 * 2 + k % 2) for k in range(COLS)]


SWAP_CORE = [(k, k ^ 1) for k in range(COLS)]


def rows_to_cols():
    pairs = []
    for i in range(ROWS):
        for j in range(COLS):
            slot, quarter = j // 4, j % 4
            pairs.append((i * COLS + j, (slot // 4 * 4 + quarter) * COLS + slot % 4 * 8 + i))
    return pairs


def cols_to_rows():
    pairs = []
    for i in range(ROWS):
        for j in range(COLS):
            pairs.append((i * COLS + j, j % 8 * COLS + j // 8 * 8 + i))
    return pairs


def gather_col(piece):
    others = [lax.ppermute(piece, "col", shift_zhi(s)) for s in (1, 3, 2)]
    quad = jnp.concatenate([piece, others[0], others[2], others[1]], 0)
    near = lax.ppermute(quad, "col", shift_x(1)), lax.ppermute(quad, "col", shift_x(3))
    far = lax.ppermute(quad, "col", shift_x(2))
    own = [quad, near[0], far, near[1]]
    return own + [lax.ppermute(q, "col", SWAP_CORE) for q in own]


def gather_row(piece):
    return [piece] + [lax.ppermute(piece, "row", shift_row(s)) for s in range(1, ROWS)]


def col_position():
    j = lax.axis_index("col")
    return j // 8, j // 2 % 4, j % 2


def chunk_copies(pieces, target, sem, chunk_of):
    zhi, x, core = col_position()
    copies = []
    for dc in range(2):
        for dx in range(4):
            for dz in range(4):
                c = chunk_of((zhi + 4 - dz) % 4, (x + 4 - dx) % 4, (core + dc) % 2)
                copies.append(
                    pltpu.make_async_copy(
                        pieces[dc * 4 + dx].at[pl.ds(dz * CH, CH)],
                        target.at[pl.ds(pl.multiple_of(c * CH, CH), CH)],
                        sem,
                    )
                )
    return copies


def v_chunk(zhi, x, core):
    return zhi * 8 + x * 2 + core


def y_chunk(zhi, x, core):
    k = x * 2 + core
    return zhi * 4 + k // 4 * 16 + k % 4


def row_copies(pieces, first, count, target, sem):
    i = lax.axis_index("row")
    copies = []
    for s in range(ROWS):
        k = (i + ROWS - s) % ROWS
        copies.append(
            pltpu.make_async_copy(
                pieces[s].at[pl.ds(first, count)],
                target.at[pl.ds(pl.multiple_of(k * count, count), count)],
                sem,
            )
        )
    return copies


def first_kernel(a_ref, *refs):
    pieces, out_ref, v_all, acc, gram, sem = refs[:8], refs[8], *refs[9:]
    step = pl.program_id(0)
    rows = a_ref.shape[0]

    @pl.when(step == 0)
    def _():
        copies = chunk_copies(pieces, v_all, sem, v_chunk)
        for c in copies:
            c.start()
        for c in copies:
            c.wait()

    v = v_all[pl.ds(pl.multiple_of(step * rows, rows), rows), :]
    ah, al = split(a_ref[...])
    vh, vl = split(v)

    def dot(a, b):
        return lax.dot_general(a, b, (TN, ((), ())), preferred_element_type=F32)

    part = dot(ah, vl) + dot(al, vh) + dot(ah, vh)
    g = dot(vh[:, :256], vl[:, 256:]) + dot(vl[:, :256], vh[:, 256:]) + dot(vh[:, :256], vh[:, 256:])

    @pl.when(step == 0)
    def _():
        acc[...] = part
        gram[...] = g

    @pl.when(step > 0)
    def _():
        acc[...] += part
        gram[...] += g

    @pl.when(step == pl.num_programs(0) - 1)
    def _():
        for k in range(ROWS):
            out_ref[k, :CH, :] = acc[k * CH:(k + 1) * CH, :]
            out_ref[k, CH:, :256] = gram[k * 16:(k + 1) * 16, :]
            out_ref[k, CH:, 256:] = gram[128 + k * 16:128 + (k + 1) * 16, :]


def first_call(a_tiles, pieces):
    blk = 512
    return pl.pallas_call(
        first_kernel,
        grid=(2048 // blk,),
        in_specs=[pl.BlockSpec((blk, W2), lambda s: (s, 0))] + [pl.BlockSpec(memory_space=ANY)] * 8,
        out_specs=pl.BlockSpec((ROWS, CH + 16, W2), lambda s: (0, 0, 0)),
        out_shape=jax.ShapeDtypeStruct((ROWS, CH + 16, W2), F32),
        scratch_shapes=[
            pltpu.VMEM((2048, W2), F32),
            pltpu.VMEM((W2, W2), F32),
            pltpu.VMEM((256, 256), F32),
            pltpu.SemaphoreType.DMA(()),
        ],
        name="first_product",
    )(a_tiles, *pieces)


def gram_kernel(*refs):
    vp, yp = refs[:8], refs[8:16]
    out_ref, v_all, y_all, full, sem = refs[16:]
    copies = row_copies(vp, 0, CH, v_all, sem) + row_copies(yp, 0, CH, y_all, sem)
    for c in copies:
        c.start()
    for c in copies:
        c.wait()
    full[...] = mm3(v_all[...], y_all[...], TN)
    i = lax.axis_index("row")
    out_ref[...] = full[pl.ds(pl.multiple_of(i * CH, CH), CH), :]


def gram_call(v_pieces, y_pieces):
    return pl.pallas_call(
        gram_kernel,
        in_specs=[pl.BlockSpec(memory_space=ANY)] * 16,
        out_specs=pl.BlockSpec(memory_space=pltpu.VMEM),
        out_shape=jax.ShapeDtypeStruct((CH, W2), F32),
        scratch_shapes=[
            pltpu.VMEM((W2, W2), F32),
            pltpu.VMEM((W2, W2), F32),
            pltpu.VMEM((W2, W2), F32),
            pltpu.SemaphoreType.DMA(()),
        ],
        name="projected_share",
    )(*v_pieces, *y_pieces)


def right_kernel(*refs):
    t_ref, vp, yp = refs[0], refs[1:9], refs[9:17]
    t_out, right_out, yt_out, v_all, y_all, g_all, sem = refs[17:]
    copies = (
        row_copies(vp, 0, CH, v_all, sem)
        + row_copies(yp, 0, CH, y_all, sem)
        + row_copies(yp, CH, 16, g_all, sem)
    )
    for c in copies:
        c.start()
    for c in copies:
        c.wait()
    t1, t2 = t_ref[0], t_ref[1]
    cross = jnp.concatenate([g_all[:, :256], g_all[:, 256:]], 0)
    corner = -mm3(mm3(t1, cross, NN), t2, NN)
    t = jnp.concatenate(
        [jnp.concatenate([t1, corner], 1), jnp.concatenate([jnp.zeros_like(t2), t2], 1)], 0
    )
    t_out[...] = t
    right_out[...] = mm3(v_all[...], t, NT)
    yt_out[...] = mm3(y_all[...], t, NN)


def right_call(t_blocks, v_pieces, y_pieces):
    vmem = pl.BlockSpec(memory_space=pltpu.VMEM)
    square = jax.ShapeDtypeStruct((W2, W2), F32)
    return pl.pallas_call(
        right_kernel,
        in_specs=[vmem] + [pl.BlockSpec(memory_space=ANY)] * 16,
        out_specs=[vmem] * 3,
        out_shape=[square] * 3,
        scratch_shapes=[
            pltpu.VMEM((W2, W2), F32),
            pltpu.VMEM((W2, W2), F32),
            pltpu.VMEM((128, W2), F32),
            pltpu.SemaphoreType.DMA(()),
        ],
        name="right_factors",
    )(t_blocks, *v_pieces, *y_pieces)


def last_kernel(a_ref, t_ref, right_ref, yt_ref, *refs):
    vp, yp, pp = refs[:8], refs[8:16], refs[16:24]
    out_ref, w_ref, left, p_all, rh, rl, sem = refs[24:]
    step = pl.program_id(0)
    rows = a_ref.shape[0]

    @pl.when(step == 0)
    def _():
        copies = (
            row_copies(pp, 0, CH, p_all, sem)
            + chunk_copies(yp, left.at[0], sem, y_chunk)
            + chunk_copies(vp, left.at[1], sem, v_chunk)
        )
        for c in copies:
            c.start()
        for c in copies:
            c.wait()
        t = t_ref[...]
        pt = mm3(p_all[...], t, NN)
        right = right_ref[...]
        rh[:, :W2], rl[:, :W2] = split(right)
        rh[:, W2:], rl[:, W2:] = split(yt_ref[...] - mm3(right, pt, NN))
        mine = pl.ds(pl.multiple_of(lax.axis_index("col") * CH, CH), CH)
        vt = mm3(left[1, mine, :], t, NT)
        w_ref[...] = mm3(left[0, mine, :], t, NN) - 0.5 * mm3(vt, pt, NN)

    here = pl.ds(pl.multiple_of(step * rows, rows), rows)

    def dot(a, b):
        return lax.dot_general(a, b, (NT, ((), ())), preferred_element_type=F32)

    yh, yl = split(left[0, here, :])
    vh, vl = split(left[1, here, :])
    lh = jnp.concatenate([yh, vh], 1)
    ll = jnp.concatenate([yl, vl], 1)
    out_ref[...] = a_ref[...] - (dot(lh, rl[...]) + dot(ll, rh[...]) + dot(lh, rh[...]))


def last_call(a_tiles, t, right, yt, v_pieces, y_pieces, p_pieces):
    blk = 256
    vmem = pl.BlockSpec(memory_space=pltpu.VMEM)
    return pl.pallas_call(
        last_kernel,
        grid=(2048 // blk,),
        in_specs=[pl.BlockSpec((blk, W2), lambda s: (s, 0))]
        + [vmem] * 3
        + [pl.BlockSpec(memory_space=ANY)] * 24,
        out_specs=[pl.BlockSpec((blk, W2), lambda s: (s, 0)), pl.BlockSpec((CH, W2), lambda s: (0, 0))],
        out_shape=[
            jax.ShapeDtypeStruct((2048, W2), F32),
            jax.ShapeDtypeStruct((CH, W2), F32),
        ],
        scratch_shapes=[
            pltpu.VMEM((2, 2048, W2), F32),
            pltpu.VMEM((W2, W2), F32),
            pltpu.VMEM((W2, 2 * W2), BF16),
            pltpu.VMEM((W2, 2 * W2), BF16),
            pltpu.SemaphoreType.DMA(()),
        ],
        name="final_update",
    )(a_tiles, t, right, yt, *v_pieces, *y_pieces, *p_pieces)


def body(a_tiles, reflectors, t_blocks):
    v_pieces = gather_col(reflectors)
    v_share = lax.ppermute(reflectors, ("row", "col"), rows_to_cols())
    vc_pieces = gather_row(v_share)
    partial = first_call(a_tiles, v_pieces)
    received = lax.all_to_all(partial, "row", 0, 0, tiled=True)
    y_share = jnp.sum(received, axis=0)
    y_own = lax.ppermute(y_share[:CH], ("row", "col"), cols_to_rows())
    y_pieces = gather_col(y_own)
    yc_pieces = gather_row(y_share)
    p_share = gram_call(vc_pieces, yc_pieces)
    p_share = p_share + lax.ppermute(p_share, "col", SWAP_CORE)
    p_share = p_share + sum(lax.ppermute(p_share, "col", shift_x(s)) for s in (1, 2, 3))
    p_share = p_share + sum(lax.ppermute(p_share, "col", shift_zhi(s)) for s in (1, 2, 3))
    p_pieces = gather_row(p_share)
    t, right, yt = right_call(t_blocks, vc_pieces, yc_pieces)
    updated, w_piece = last_call(a_tiles, t, right, yt, v_pieces, y_pieces, p_pieces)
    return (updated, w_piece)


def solution(mesh):
    placed = (P("row", "col"), P(("row", "col"), None), P())
    return jax.shard_map(
        body,
        mesh=mesh,
        in_specs=placed,
        out_specs=(P("row", "col"), P(("row", "col"), None)),
        check_vma=False,
    )
```

```python
import jax
import jax.numpy as jnp
from jax import lax
from jax.experimental import pallas as pl
from jax.experimental.pallas import tpu as pltpu
from jax.sharding import PartitionSpec as P


ROWS = 8
COLS = 32
CH = 64
QUAD = 4 * CH
W2 = 512
F32 = jnp.float32
BF16 = jnp.bfloat16
HBM = pl.BlockSpec(memory_space=pl.ANY)
VMEM = pl.BlockSpec(memory_space=pltpu.VMEM)


NN = ((1,), (0,))
NT = ((1,), (1,))
TN = ((0,), (0,))


def split(value):
    high = value.astype(BF16)
    low = (value - high.astype(F32)).astype(BF16)
    return high, low


def dot(left, right, dims):
    return lax.dot_general(left, right, (dims, ((), ())), preferred_element_type=F32)


def stack_left(value, axis):
    high, low = split(value)
    return jnp.concatenate([high, low, high], axis)


def stack_right(value, axis):
    high, low = split(value)
    return jnp.concatenate([low, high, high], axis)


def mm3(left, right, dims):
    return dot(stack_left(left, dims[0][0]), stack_right(right, dims[1][0]), dims)


def shift_zhi(s):
    return [(k, (k // 8 + s) % 4 * 8 + k % 8) for k in range(COLS)]


def shift_x(s):
    return [(k, k // 8 * 8 + (k // 2 % 4 + s) % 4 * 2 + k % 2) for k in range(COLS)]


SWAP_CORE = [(k, k ^ 1) for k in range(COLS)]


def rows_to_cols():
    pairs = []
    for i in range(ROWS):
        for j in range(COLS):
            slot, quarter = j // 4, j % 4
            pairs.append((i * COLS + j, (slot // 4 * 4 + quarter) * COLS + slot % 4 * 8 + i))
    return pairs


def cols_to_rows():
    pairs = []
    for i in range(ROWS):
        for j in range(COLS):
            pairs.append((i * COLS + j, j % 8 * COLS + j // 8 * 8 + i))
    return pairs


def swap(value):
    return lax.ppermute(value, "col", SWAP_CORE)


SWAP_ZLO = [(k, k ^ 1) for k in range(ROWS)]


def shift_y(s):
    return [(k, (k // 2 + s) % 4 * 2 + k % 2) for k in range(ROWS)]


def row_spread(piece):
    pair = jnp.stack([piece, lax.ppermute(piece, "row", SWAP_ZLO)])
    moved = {s: lax.ppermute(pair, "row", shift_y(s)) for s in (2, 1, 3)}
    return [pair] + [moved[s] for s in (1, 2, 3)]


def groups_of(key):
    found = {}
    for k in range(COLS):
        found.setdefault(key(k), []).append(k)
    return list(found.values())


Z_GROUPS = groups_of(lambda k: k % 8)
X_GROUPS = groups_of(lambda k: (k // 8, k % 2))


def exchange(value):
    return lax.all_to_all(value, "row", 0, 0, tiled=True)


def row_gather(piece):
    return exchange(jnp.broadcast_to(piece[None], (ROWS,) + piece.shape))


def group_gather(piece, groups):
    value = jnp.broadcast_to(piece[None], (4,) + piece.shape)
    return lax.all_to_all(value, "col", 0, 0, axis_index_groups=groups, tiled=True)


def spread_x(quad):
    left = lax.ppermute(quad, "col", shift_x(1))
    right = lax.ppermute(quad, "col", shift_x(3))
    low = lax.ppermute(left[: QUAD // 2], "col", shift_x(1))
    high = lax.ppermute(right[QUAD // 2:], "col", shift_x(3))
    near = [quad, left, right]
    near = near + [swap(q) for q in near]
    far = [low, high]
    far = far + [swap(q) for q in far]
    return near, far


def col_position():
    j = lax.axis_index("col")
    return j // 8, j // 2 % 4, j % 2


def source_of(q, dz):
    zhi, x, core = col_position()
    is_far = q >= 6
    dc = jnp.where(is_far, q - 6, q // 3)
    turn = q % 3
    dx = jnp.where(is_far, 2, jnp.where(turn == 2, 3, turn))
    return (zhi + 4 - dz) % 4, (x + 4 - dx) % 4, (core + dc) % 2


def v_chunk(q, dz):
    zhi, x, core = source_of(q, dz)
    return zhi * 8 + x * 2 + core


def chunk_rows(c):
    return pl.ds(pl.multiple_of(c * CH, CH), CH)


def load_quads(near, far, first, target, sems):
    for q, ref in enumerate(near):
        pltpu.make_async_copy(ref, target.at[q + first], sems.at[q + first]).start()
    half = QUAD // 2
    for n, ref in enumerate(far):
        q = len(near) + n // 2 + first
        rows = pl.ds(n % 2 * half, half)
        pltpu.make_async_copy(ref, target.at[q, rows], sems.at[q]).start()


def load_chunks(source, target, sems, quads, first, chunk_of):
    def one(q, carry):
        for dz in range(4):
            pltpu.make_async_copy(
                source.at[chunk_rows(chunk_of(q + first, dz))],
                target.at[q, pl.ds(dz * CH, CH)],
                sems.at[q],
            ).start()
        return carry

    lax.fori_loop(0, quads, one, 0)


def wait_quad(target, sems, q):
    pltpu.make_async_copy(target.at[q], target.at[q], sems.at[q]).wait()


def near_kernel(a_ref, *refs):
    near, refs = refs[:6], refs[6:]
    acc, gram, a_all, v_all, a_sems, v_sems = refs
    load_quads(near, [], 0, v_all, v_sems)
    load_chunks(a_ref, a_all, a_sems, 6, 0, v_chunk)
    acc[...] = jnp.zeros_like(acc)
    gram[...] = jnp.zeros_like(gram)

    def one(q, carry):
        wait_quad(v_all, v_sems, q)
        wait_quad(a_all, a_sems, q)
        left = stack_left(a_all[q], 0)
        v = v_all[q]
        right = stack_right(v, 0)
        acc[...] += dot(left, right, TN)
        gram[...] += dot(stack_left(v[:, :256], 0), right[:, 256:], TN)
        return carry

    lax.fori_loop(0, 6, one, 0)


def near_call(a_tiles, near):
    return pl.pallas_call(
        near_kernel,
        in_specs=[HBM] * 7,
        out_specs=[VMEM] * 2,
        out_shape=[jax.ShapeDtypeStruct((W2, W2), F32), jax.ShapeDtypeStruct((256, 256), F32)],
        scratch_shapes=[
            pltpu.VMEM((6, QUAD, W2), F32),
            pltpu.VMEM((6, QUAD, W2), F32),
            pltpu.SemaphoreType.DMA((6,)),
            pltpu.SemaphoreType.DMA((6,)),
        ],
        name="first_near",
    )(a_tiles, *near)


def far_kernel(a_ref, acc_ref, gram_ref, *refs):
    far, refs = refs[:4], refs[4:]
    out_ref, a_all, v_all, a_sems, v_sems = refs
    load_quads([], far, 0, v_all, v_sems)
    load_chunks(a_ref, a_all, a_sems, 2, 6, v_chunk)
    for q in range(2):
        wait_quad(v_all, v_sems, q)
        wait_quad(a_all, a_sems, q)
    v = v_all[...].reshape(2 * QUAD, W2)
    right = stack_right(v, 0)
    left_v = stack_left(v[:, :256], 0)
    gram = gram_ref[...] + dot(left_v, right[:, 256:], TN)
    acc = dot(stack_left(a_all[...].reshape(2 * QUAD, W2), 0), right, TN)
    for k in range(ROWS):
        rows = slice(k * CH, (k + 1) * CH)
        out_ref[k, :CH, :] = acc_ref[rows, :] + acc[rows, :]
        out_ref[k, CH:, :256] = gram[k * 16:(k + 1) * 16, :]
        out_ref[k, CH:, 256:] = gram[128 + k * 16:128 + (k + 1) * 16, :]


def far_call(a_tiles, acc, gram, far):
    return pl.pallas_call(
        far_kernel,
        in_specs=[HBM] + [VMEM] * 2 + [HBM] * 4,
        out_specs=VMEM,
        out_shape=jax.ShapeDtypeStruct((ROWS, CH + 16, W2), F32),
        scratch_shapes=[
            pltpu.VMEM((2, QUAD, W2), F32),
            pltpu.VMEM((2, QUAD, W2), F32),
            pltpu.SemaphoreType.DMA((2,)),
            pltpu.SemaphoreType.DMA((2,)),
        ],
        name="first_far",
    )(a_tiles, acc, gram, *far)


def share_kernel(v_ref, part_ref, keep_ref, send_ref, full):
    core = lax.axis_index("col") % 2
    z = part_ref[:, :CH, :].reshape(W2, W2)
    full[...] = mm3(v_ref[...].reshape(W2, W2), z, TN).reshape(ROWS, CH, W2)
    half = CH // 2
    keep_ref[...] = full[:, pl.ds(pl.multiple_of(core * half, half), half), :]
    send_ref[...] = full[:, pl.ds(pl.multiple_of((1 - core) * half, half), half), :]


def share_call(v_cols, partial):
    half = jax.ShapeDtypeStruct((ROWS, CH // 2, W2), F32)
    return pl.pallas_call(
        share_kernel,
        in_specs=[VMEM] * 2,
        out_specs=[VMEM] * 2,
        out_shape=[half] * 2,
        scratch_shapes=[pltpu.VMEM((ROWS, CH, W2), F32)],
        name="projected_share",
    )(v_cols, partial)


def right_kernel(t_ref, v_ref, own_ref, *refs):
    pairs = refs[:4]
    t_out, stack_out, yt_out, vt_out, y_rows, g_rows = refs[4:]
    i = lax.axis_index("row")
    for n in range(ROWS):
        row = (i // 2 + 4 - n // 2) % 4 * 2 + (i + n) % 2
        y_rows[row] = pairs[n // 2][n % 2, :CH, :]
        g_rows[row] = pairs[n // 2][n % 2, CH:, :]
    t1, t2 = t_ref[0], t_ref[1]
    g = g_rows[...].reshape(128, W2)
    cross = jnp.concatenate([g[:, :256], g[:, 256:]], 0)
    t_out[:256, :256] = t1
    t_out[256:, :256] = jnp.zeros_like(t1)
    t_out[256:, 256:] = t2
    t_out[:256, 256:] = -mm3(mm3(t1, cross, NN), t2, NN)
    t = t_out[...]
    vt_out[...] = mm3(own_ref[...], t, NT)
    put_stack(stack_out, mm3(t, v_ref[...], NT))
    yt_out[...] = mm3(y_rows[...].reshape(W2, W2), t, NN).T


def put_stack(target, value):
    high, low = split(value)
    target[:W2, :] = low
    target[W2:2 * W2, :] = high
    target[2 * W2:, :] = high


def right_call(t_blocks, v_cols, own, pairs):
    square = jax.ShapeDtypeStruct((W2, W2), F32)
    return pl.pallas_call(
        right_kernel,
        in_specs=[VMEM] * 7,
        out_specs=[VMEM] * 4,
        out_shape=[
            square,
            jax.ShapeDtypeStruct((3 * W2, W2), BF16),
            square,
            jax.ShapeDtypeStruct((CH, W2), F32),
        ],
        scratch_shapes=[
            pltpu.VMEM((ROWS, CH, W2), F32),
            pltpu.VMEM((ROWS, 16, W2), F32),
        ],
        name="right_factors",
    )(t_blocks, v_cols.reshape(W2, W2), own, *pairs)


def last_kernel(a_ref, t_ref, stack_ref, yt_ref, vt_ref, p_own, p_other, *refs):
    y_quads, near, far, refs = refs[:8], refs[8:14], refs[14:18], refs[18:]
    out_ref, w_ref, y_all, v_all, a_all, p_all, t_all, yt_all, vt_all, stack1, stack2 = refs[:11]
    y_sem, v_sems, a_sems, p_sems, t_sems, out_sem = refs[11:]
    zhi, x, core = col_position()
    half = CH // 2
    copies = []
    for c, ref in enumerate((p_own, p_other)):
        place = pl.ds(pl.multiple_of((core + c) % 2 * half, half), half)
        copies.append(pltpu.make_async_copy(ref, p_all.at[:, place], p_sems.at[c]))
    fixed = ((t_ref, t_all), (stack_ref, stack1), (yt_ref, yt_all), (vt_ref, vt_all))
    for n, (source, target) in enumerate(fixed):
        copies.append(pltpu.make_async_copy(source, target, t_sems.at[n]))
    for c in copies:
        c.start()
    for q, ref in enumerate(y_quads):
        k = (x + 4 - q % 4) % 4 * 2 + (core + q // 4) % 2
        for dz in range(4):
            place = chunk_rows((zhi + 4 - dz) % 4 * 4 + k // 4 * 16 + k % 4)
            pltpu.make_async_copy(ref.at[pl.ds(dz * CH, CH)], y_all.at[place], y_sem).start()
    block = 512

    def block_rows(dz):
        return pl.ds(pl.multiple_of((zhi + 4 - dz) % 4 * block, block), block)

    for dz in range(4):
        for q in range(8):
            ref = near[q] if q < 6 else far[(q - 6) * 2 + dz // 2]
            source = dz * CH if q < 6 else dz % 2 * CH
            pltpu.make_async_copy(
                ref.at[pl.ds(source, CH)], v_all.at[chunk_rows(v_chunk(q, dz))], v_sems.at[dz]
            ).start()
        rows = block_rows(dz)
        pltpu.make_async_copy(a_ref.at[rows], a_all.at[rows], a_sems.at[dz]).start()
    for c in copies:
        c.wait()
    t_nn = stack_right(t_all[...], 0)
    pt = dot(stack_left(p_all[...].reshape(W2, W2), 1), t_nn, NN)
    put_stack(stack2, yt_all[...] - dot(stack_left(pt, 0), stack1[...], TN))
    w_ref[...] = -0.5 * dot(stack_left(vt_all[...], 1), stack_right(pt, 0), NN)
    pltpu.make_async_copy(y_all, y_all, y_sem).wait()
    own = y_all[chunk_rows(lax.axis_index("col")), :]
    w_ref[...] += dot(stack_left(own, 1), t_nn, NN)

    def update(dz, carry):
        rows = block_rows(dz)
        pltpu.make_async_copy(v_all.at[rows], v_all.at[rows], v_sems.at[dz]).wait()
        pltpu.make_async_copy(a_all.at[rows], a_all.at[rows], a_sems.at[dz]).wait()
        change = dot(stack_left(y_all[rows, :], 1), stack1[...], NN)
        change = change + dot(stack_left(v_all[rows, :], 1), stack2[...], NN)
        a_all[rows, :] = a_all[rows, :] - change
        pltpu.make_async_copy(a_all.at[rows], out_ref.at[rows], out_sem).start()
        return carry

    lax.fori_loop(0, 4, update, 0)
    pltpu.make_async_copy(a_all, a_all, out_sem).wait()


def last_call(a_tiles, t, stack, yt, vt, p_own, p_other, y_quads, near, far):
    return pl.pallas_call(
        last_kernel,
        in_specs=[HBM] * 25,
        out_specs=[HBM, VMEM],
        out_shape=[jax.ShapeDtypeStruct((2048, W2), F32), jax.ShapeDtypeStruct((CH, W2), F32)],
        scratch_shapes=[
            pltpu.VMEM((2048, W2), F32),
            pltpu.VMEM((2048, W2), F32),
            pltpu.VMEM((2048, W2), F32),
            pltpu.VMEM((ROWS, CH, W2), F32),
            pltpu.VMEM((W2, W2), F32),
            pltpu.VMEM((W2, W2), F32),
            pltpu.VMEM((CH, W2), F32),
            pltpu.VMEM((3 * W2, W2), BF16),
            pltpu.VMEM((3 * W2, W2), BF16),
            pltpu.SemaphoreType.DMA(()),
            pltpu.SemaphoreType.DMA((4,)),
            pltpu.SemaphoreType.DMA((4,)),
            pltpu.SemaphoreType.DMA((2,)),
            pltpu.SemaphoreType.DMA((4,)),
            pltpu.SemaphoreType.DMA(()),
        ],
        name="final_update",
    )(a_tiles, t, stack, yt, vt, p_own, p_other, *y_quads, *near, *far)


def steps(a_tiles, reflectors, t_blocks):
    from_z = {s: lax.ppermute(reflectors, "col", shift_zhi(s)) for s in (2, 1, 3)}
    v_share = lax.ppermute(reflectors, ("row", "col"), rows_to_cols())
    v_quad = jnp.concatenate([reflectors] + [from_z[s] for s in (1, 2, 3)], 0)
    v_near, v_far = spread_x(v_quad)
    v_cols = row_gather(v_share)
    acc, gram = near_call(a_tiles, v_near)
    partial = far_call(a_tiles, acc, gram, v_far)
    received = exchange(partial)
    p_keep, p_send = share_call(v_cols, partial)
    p_rows = p_keep + swap(p_send)
    y_share = jnp.sum(received, axis=0)
    y_own = lax.ppermute(y_share[:CH], ("row", "col"), cols_to_rows())
    moved = {s: lax.ppermute(y_own, "col", shift_zhi(s)) for s in (2, 1, 3)}
    y_quad = jnp.concatenate([y_own] + [moved[s] for s in (1, 2, 3)], 0)
    p_half = jnp.sum(exchange(p_rows), axis=0)
    p_half = jnp.sum(group_gather(p_half, X_GROUPS), axis=0)
    moved = {s: lax.ppermute(y_quad, "col", shift_x(s)) for s in (2, 1, 3)}
    y_quads = [y_quad] + [moved[s] for s in (1, 2, 3)]
    y_quads = y_quads + [swap(q) for q in y_quads]
    y_pairs = row_spread(y_share)
    p_half = jnp.sum(group_gather(p_half, Z_GROUPS), axis=0)
    t, stack, yt, vt = right_call(t_blocks, v_cols, reflectors, y_pairs)
    p_own = row_gather(p_half)
    p_other = swap(p_own)
    updated, w_piece = last_call(a_tiles, t, stack, yt, vt, p_own, p_other, y_quads, v_near, v_far)
    return (updated, w_piece)


def solution(mesh):
    placed = (P("row", "col"), P(("row", "col"), None), P())
    return jax.shard_map(
        steps,
        mesh=mesh,
        in_specs=placed,
        out_specs=(P("row", "col"), P(("row", "col"), None)),
        check_vma=False,
    )
```

```python
import jax
import jax.numpy as jnp
from jax import lax
from jax.experimental import pallas as pl
from jax.experimental.pallas import tpu as pltpu
from jax.sharding import PartitionSpec as P


ROWS = 8
COLS = 32
CH = 64
QUAD = 4 * CH
W2 = 512
F32 = jnp.float32
BF16 = jnp.bfloat16
HBM = pl.BlockSpec(memory_space=pl.ANY)
VMEM = pl.BlockSpec(memory_space=pltpu.VMEM)


NN = ((1,), (0,))
NT = ((1,), (1,))
TN = ((0,), (0,))


def split(value):
    high = value.astype(BF16)
    low = (value - high.astype(F32)).astype(BF16)
    return high, low


def dot(left, right, dims):
    return lax.dot_general(left, right, (dims, ((), ())), preferred_element_type=F32)


def stack_left(value, axis):
    high, low = split(value)
    return jnp.concatenate([high, low, high], axis)


def stack_right(value, axis):
    high, low = split(value)
    return jnp.concatenate([low, high, high], axis)


def mm3(left, right, dims):
    return dot(stack_left(left, dims[0][0]), stack_right(right, dims[1][0]), dims)


def shift_zhi(s):
    return [(k, (k // 8 + s) % 4 * 8 + k % 8) for k in range(COLS)]


def shift_x(s):
    return [(k, k // 8 * 8 + (k // 2 % 4 + s) % 4 * 2 + k % 2) for k in range(COLS)]


SWAP_CORE = [(k, k ^ 1) for k in range(COLS)]


def rows_to_cols():
    pairs = []
    for i in range(ROWS):
        for j in range(COLS):
            slot, quarter = j // 4, j % 4
            pairs.append((i * COLS + j, (slot // 4 * 4 + quarter) * COLS + slot % 4 * 8 + i))
    return pairs


def cols_to_rows():
    pairs = []
    for i in range(ROWS):
        for j in range(COLS):
            pairs.append((i * COLS + j, j % 8 * COLS + j // 8 * 8 + i))
    return pairs


def swap(value):
    return lax.ppermute(value, "col", SWAP_CORE)


SWAP_ZLO = [(k, k ^ 1) for k in range(ROWS)]


def shift_y(s):
    return [(k, (k // 2 + s) % 4 * 2 + k % 2) for k in range(ROWS)]


def row_spread(piece):
    pair = jnp.stack([piece, lax.ppermute(piece, "row", SWAP_ZLO)])
    moved = {s: lax.ppermute(pair, "row", shift_y(s)) for s in (2, 1, 3)}
    return [pair] + [moved[s] for s in (1, 2, 3)]


def exchange(value):
    return lax.all_to_all(value, "row", 0, 0, tiled=True)


def row_gather(piece):
    return exchange(jnp.broadcast_to(piece[None], (ROWS,) + piece.shape))


def total(value, masks):
    for mask in masks:
        other = lax.ppermute(value, "col", [(k, k ^ mask) for k in range(COLS)])
        value = value + other
    return value


def spread_x(quad):
    left = lax.ppermute(quad, "col", shift_x(1))
    right = lax.ppermute(quad, "col", shift_x(3))
    low = lax.ppermute(left[: QUAD // 2], "col", shift_x(1))
    high = lax.ppermute(right[QUAD // 2:], "col", shift_x(3))
    near = [quad, left, right]
    near = near + [swap(q) for q in near]
    far = [low, high]
    far = far + [swap(q) for q in far]
    return near, far


def col_position():
    j = lax.axis_index("col")
    return j // 8, j // 2 % 4, j % 2


def source_of(q, dz):
    zhi, x, core = col_position()
    is_far = q >= 6
    dc = jnp.where(is_far, q - 6, q // 3)
    turn = q % 3
    dx = jnp.where(is_far, 2, jnp.where(turn == 2, 3, turn))
    return (zhi + 4 - dz) % 4, (x + 4 - dx) % 4, (core + dc) % 2


def v_chunk(q, dz):
    zhi, x, core = source_of(q, dz)
    return zhi * 8 + x * 2 + core


def chunk_rows(c):
    return pl.ds(pl.multiple_of(c * CH, CH), CH)


def load_quads(near, far, first, target, sems):
    for q, ref in enumerate(near):
        pltpu.make_async_copy(ref, target.at[q + first], sems.at[q + first]).start()
    half = QUAD // 2
    for n, ref in enumerate(far):
        q = len(near) + n // 2 + first
        rows = pl.ds(n % 2 * half, half)
        pltpu.make_async_copy(ref, target.at[q, rows], sems.at[q]).start()


def load_chunks(source, target, sems, quads, first, chunk_of):
    def one(q, carry):
        for dz in range(4):
            pltpu.make_async_copy(
                source.at[chunk_rows(chunk_of(q + first, dz))],
                target.at[q, pl.ds(dz * CH, CH)],
                sems.at[q],
            ).start()
        return carry

    lax.fori_loop(0, quads, one, 0)


def wait_quad(target, sems, q):
    pltpu.make_async_copy(target.at[q], target.at[q], sems.at[q]).wait()


def near_kernel(a_ref, *refs):
    near, refs = refs[:6], refs[6:]
    acc, gram, a_all, v_all, a_sems, v_sems = refs
    load_quads(near, [], 0, v_all, v_sems)
    load_chunks(a_ref, a_all, a_sems, 6, 0, v_chunk)
    acc[...] = jnp.zeros_like(acc)
    gram[...] = jnp.zeros_like(gram)

    def one(q, carry):
        wait_quad(v_all, v_sems, q)
        wait_quad(a_all, a_sems, q)
        left = stack_left(a_all[q], 0)
        v = v_all[q]
        right = stack_right(v, 0)
        acc[...] += dot(left, right, TN)
        gram[...] += dot(stack_left(v[:, :256], 0), right[:, 256:], TN)
        return carry

    lax.fori_loop(0, 6, one, 0)


def near_call(a_tiles, near):
    return pl.pallas_call(
        near_kernel,
        in_specs=[HBM] * 7,
        out_specs=[VMEM] * 2,
        out_shape=[jax.ShapeDtypeStruct((W2, W2), F32), jax.ShapeDtypeStruct((256, 256), F32)],
        scratch_shapes=[
            pltpu.VMEM((6, QUAD, W2), F32),
            pltpu.VMEM((6, QUAD, W2), F32),
            pltpu.SemaphoreType.DMA((6,)),
            pltpu.SemaphoreType.DMA((6,)),
        ],
        name="first_near",
    )(a_tiles, *near)


def far_kernel(a_ref, acc_ref, gram_ref, *refs):
    far, refs = refs[:4], refs[4:]
    out_ref, a_all, v_all, a_sems, v_sems = refs
    load_quads([], far, 0, v_all, v_sems)
    load_chunks(a_ref, a_all, a_sems, 2, 6, v_chunk)
    for q in range(2):
        wait_quad(v_all, v_sems, q)
        wait_quad(a_all, a_sems, q)
    v = v_all[...].reshape(2 * QUAD, W2)
    right = stack_right(v, 0)
    left_v = stack_left(v[:, :256], 0)
    gram = gram_ref[...] + dot(left_v, right[:, 256:], TN)
    acc = dot(stack_left(a_all[...].reshape(2 * QUAD, W2), 0), right, TN)
    for k in range(ROWS):
        rows = slice(k * CH, (k + 1) * CH)
        out_ref[k, :CH, :] = acc_ref[rows, :] + acc[rows, :]
        out_ref[k, CH:, :256] = gram[k * 16:(k + 1) * 16, :]
        out_ref[k, CH:, 256:] = gram[128 + k * 16:128 + (k + 1) * 16, :]


def far_call(a_tiles, acc, gram, far):
    return pl.pallas_call(
        far_kernel,
        in_specs=[HBM] + [VMEM] * 2 + [HBM] * 4,
        out_specs=VMEM,
        out_shape=jax.ShapeDtypeStruct((ROWS, CH + 16, W2), F32),
        scratch_shapes=[
            pltpu.VMEM((2, QUAD, W2), F32),
            pltpu.VMEM((2, QUAD, W2), F32),
            pltpu.SemaphoreType.DMA((2,)),
            pltpu.SemaphoreType.DMA((2,)),
        ],
        name="first_far",
    )(a_tiles, acc, gram, *far)


def share_kernel(v_ref, part_ref, keep_ref, send_ref, full):
    core = lax.axis_index("col") % 2
    z = part_ref[:, :CH, :].reshape(W2, W2)
    full[...] = mm3(v_ref[...].reshape(W2, W2), z, TN).reshape(ROWS, CH, W2)
    half = CH // 2
    keep_ref[...] = full[:, pl.ds(pl.multiple_of(core * half, half), half), :]
    send_ref[...] = full[:, pl.ds(pl.multiple_of((1 - core) * half, half), half), :]


def share_call(v_cols, partial):
    half = jax.ShapeDtypeStruct((ROWS, CH // 2, W2), F32)
    return pl.pallas_call(
        share_kernel,
        in_specs=[VMEM] * 2,
        out_specs=[VMEM] * 2,
        out_shape=[half] * 2,
        scratch_shapes=[pltpu.VMEM((ROWS, CH, W2), F32)],
        name="projected_share",
    )(v_cols, partial)


def right_kernel(t_ref, v_ref, own_ref, *refs):
    pairs = refs[:4]
    t_out, stack_out, yt_out, vt_out, y_rows, g_rows = refs[4:]
    i = lax.axis_index("row")
    for n in range(ROWS):
        row = (i // 2 + 4 - n // 2) % 4 * 2 + (i + n) % 2
        y_rows[row] = pairs[n // 2][n % 2, :CH, :]
        g_rows[row] = pairs[n // 2][n % 2, CH:, :]
    t1, t2 = t_ref[0], t_ref[1]
    g = g_rows[...].reshape(128, W2)
    cross = jnp.concatenate([g[:, :256], g[:, 256:]], 0)
    t_out[:256, :256] = t1
    t_out[256:, :256] = jnp.zeros_like(t1)
    t_out[256:, 256:] = t2
    t_out[:256, 256:] = -mm3(mm3(t1, cross, NN), t2, NN)
    t = t_out[...]
    vt_out[...] = mm3(own_ref[...], t, NT)
    put_stack(stack_out, mm3(t, v_ref[...], NT))
    yt_out[...] = mm3(y_rows[...].reshape(W2, W2), t, NN).T


def put_stack(target, value):
    high, low = split(value)
    target[:W2, :] = low
    target[W2:2 * W2, :] = high
    target[2 * W2:, :] = high


def right_call(t_blocks, v_cols, own, pairs):
    square = jax.ShapeDtypeStruct((W2, W2), F32)
    return pl.pallas_call(
        right_kernel,
        in_specs=[VMEM] * 7,
        out_specs=[VMEM] * 4,
        out_shape=[
            square,
            jax.ShapeDtypeStruct((3 * W2, W2), BF16),
            square,
            jax.ShapeDtypeStruct((CH, W2), F32),
        ],
        scratch_shapes=[
            pltpu.VMEM((ROWS, CH, W2), F32),
            pltpu.VMEM((ROWS, 16, W2), F32),
        ],
        name="right_factors",
    )(t_blocks, v_cols.reshape(W2, W2), own, *pairs)


def last_kernel(a_ref, t_ref, stack_ref, yt_ref, vt_ref, p_own, p_other, *refs):
    y_quads, near, far, refs = refs[:8], refs[8:14], refs[14:18], refs[18:]
    out_ref, w_ref, y_all, v_all, a_all, p_all, t_all, yt_all, vt_all, stack1, stack2 = refs[:11]
    y_sem, v_sems, a_sems, p_sems, t_sems, out_sem = refs[11:]
    zhi, x, core = col_position()
    half = CH // 2
    copies = []
    for c, ref in enumerate((p_own, p_other)):
        place = pl.ds(pl.multiple_of((core + c) % 2 * half, half), half)
        copies.append(pltpu.make_async_copy(ref, p_all.at[:, place], p_sems.at[c]))
    fixed = ((t_ref, t_all), (stack_ref, stack1), (yt_ref, yt_all), (vt_ref, vt_all))
    for n, (source, target) in enumerate(fixed):
        copies.append(pltpu.make_async_copy(source, target, t_sems.at[n]))
    for c in copies:
        c.start()
    for q, ref in enumerate(y_quads):
        k = (x + 4 - q % 4) % 4 * 2 + (core + q // 4) % 2
        for dz in range(4):
            place = chunk_rows((zhi + 4 - dz) % 4 * 4 + k // 4 * 16 + k % 4)
            pltpu.make_async_copy(ref.at[pl.ds(dz * CH, CH)], y_all.at[place], y_sem).start()
    block = 512

    def block_rows(dz):
        return pl.ds(pl.multiple_of((zhi + 4 - dz) % 4 * block, block), block)

    for dz in range(4):
        for q in range(8):
            ref = near[q] if q < 6 else far[(q - 6) * 2 + dz // 2]
            source = dz * CH if q < 6 else dz % 2 * CH
            pltpu.make_async_copy(
                ref.at[pl.ds(source, CH)], v_all.at[chunk_rows(v_chunk(q, dz))], v_sems.at[dz]
            ).start()
        rows = block_rows(dz)
        pltpu.make_async_copy(a_ref.at[rows], a_all.at[rows], a_sems.at[dz]).start()
    for c in copies:
        c.wait()
    t_nn = stack_right(t_all[...], 0)
    pt = dot(stack_left(p_all[...].reshape(W2, W2), 1), t_nn, NN)
    put_stack(stack2, yt_all[...] - dot(stack_left(pt, 0), stack1[...], TN))
    w_ref[...] = -0.5 * dot(stack_left(vt_all[...], 1), stack_right(pt, 0), NN)
    pltpu.make_async_copy(y_all, y_all, y_sem).wait()
    own = y_all[chunk_rows(lax.axis_index("col")), :]
    w_ref[...] += dot(stack_left(own, 1), t_nn, NN)

    def update(dz, carry):
        rows = block_rows(dz)
        pltpu.make_async_copy(v_all.at[rows], v_all.at[rows], v_sems.at[dz]).wait()
        pltpu.make_async_copy(a_all.at[rows], a_all.at[rows], a_sems.at[dz]).wait()
        change = dot(stack_left(y_all[rows, :], 1), stack1[...], NN)
        change = change + dot(stack_left(v_all[rows, :], 1), stack2[...], NN)
        a_all[rows, :] = a_all[rows, :] - change
        pltpu.make_async_copy(a_all.at[rows], out_ref.at[rows], out_sem).start()
        return carry

    lax.fori_loop(0, 4, update, 0)
    pltpu.make_async_copy(a_all, a_all, out_sem).wait()


def last_call(a_tiles, t, stack, yt, vt, p_own, p_other, y_quads, near, far):
    return pl.pallas_call(
        last_kernel,
        in_specs=[HBM] * 25,
        out_specs=[HBM, VMEM],
        out_shape=[jax.ShapeDtypeStruct((2048, W2), F32), jax.ShapeDtypeStruct((CH, W2), F32)],
        scratch_shapes=[
            pltpu.VMEM((2048, W2), F32),
            pltpu.VMEM((2048, W2), F32),
            pltpu.VMEM((2048, W2), F32),
            pltpu.VMEM((ROWS, CH, W2), F32),
            pltpu.VMEM((W2, W2), F32),
            pltpu.VMEM((W2, W2), F32),
            pltpu.VMEM((CH, W2), F32),
            pltpu.VMEM((3 * W2, W2), BF16),
            pltpu.VMEM((3 * W2, W2), BF16),
            pltpu.SemaphoreType.DMA(()),
            pltpu.SemaphoreType.DMA((4,)),
            pltpu.SemaphoreType.DMA((4,)),
            pltpu.SemaphoreType.DMA((2,)),
            pltpu.SemaphoreType.DMA((4,)),
            pltpu.SemaphoreType.DMA(()),
        ],
        name="final_update",
    )(a_tiles, t, stack, yt, vt, p_own, p_other, *y_quads, *near, *far)


def steps(a_tiles, reflectors, t_blocks):
    from_z = {s: lax.ppermute(reflectors, "col", shift_zhi(s)) for s in (2, 1, 3)}
    v_share = lax.ppermute(reflectors, ("row", "col"), rows_to_cols())
    v_quad = jnp.concatenate([reflectors] + [from_z[s] for s in (1, 2, 3)], 0)
    v_near, v_far = spread_x(v_quad)
    v_cols = row_gather(v_share)
    acc, gram = near_call(a_tiles, v_near)
    partial = far_call(a_tiles, acc, gram, v_far)
    received = exchange(partial)
    p_keep, p_send = share_call(v_cols, partial)
    p_rows = p_keep + swap(p_send)
    y_share = jnp.sum(received, axis=0)
    y_own = lax.ppermute(y_share[:CH], ("row", "col"), cols_to_rows())
    moved = {s: lax.ppermute(y_own, "col", shift_zhi(s)) for s in (2, 1, 3)}
    y_quad = jnp.concatenate([y_own] + [moved[s] for s in (1, 2, 3)], 0)
    p_parts = exchange(p_rows)
    p_half = jnp.sum(p_parts, axis=0)
    p_half = total(p_half, (2, 6))
    moved = {s: lax.ppermute(y_quad, "col", shift_x(s)) for s in (2, 1, 3)}
    y_quads = [y_quad] + [moved[s] for s in (1, 2, 3)]
    y_quads = y_quads + [swap(q) for q in y_quads]
    y_pairs = row_spread(y_share)
    p_half = total(p_half, (8, 24))
    t, stack, yt, vt = right_call(t_blocks, v_cols, reflectors, y_pairs)
    p_own = row_gather(p_half)
    p_other = swap(p_own)
    updated, w_piece = last_call(a_tiles, t, stack, yt, vt, p_own, p_other, y_quads, v_near, v_far)
    return (updated, w_piece)


def solution(mesh):
    placed = (P("row", "col"), P(("row", "col"), None), P())
    return jax.shard_map(
        steps,
        mesh=mesh,
        in_specs=placed,
        out_specs=(P("row", "col"), P(("row", "col"), None)),
        check_vma=False,
    )
```
